32 devices in a mesh: row: 8 (over z, core), col: 4 (over y, x).
Axes of the slice: x: 2, y: 2, z: 4, core: 2. Of those that a mesh axis runs over, the one named last changes fastest.
Arguments:
- amplitudes: float32 [16, 16, 160, 160], P('row', 'col'), may hold values from -8 to 8, as said below
- vvvv: float32 [160, 160, 160, 160], P('row', None, 'col'), may hold values from -0.0390625 to 0.0390625
- hole_ints: float32 [16, 16, 16, 16], replicated, may hold values from -0.375 to 0.375
- exchange_ints: float32 [16, 16, 160, 160], P('row', None, 'col'), may hold values from -0.0024414062 to 0.0024414062
- fock_occ: float32 [16, 16], replicated, may hold values from -1.5 to 1.5
- fock_vir: float32 [160, 160], replicated, may hold values from -0.5 to 0.5
- eps_occ: float32 [16], replicated, may hold values from -2 to -0.5
- eps_vir: float32 [160], replicated, may hold values from 0.3 to 3
Outputs:
- update: float32 [16, 16, 160, 160], P('row', 'col')
The draws below stay inside these ranges and needn't reach their ends.
Inputs may be any that keep to these rules, and one draw needn't show every extreme that they name: amplitudes[i, j, a, b] equals amplitudes[j, i, b, a].
All inputs are finite; a program needn't handle non-finite values.
Results may differ from the reference program's by a relative error of at most 0.000064.
Values sent between devices are 32-bit elements; how exact they have to be, the bound alone decides.
A program may use at most 256 MiB of HBM per device.

```python
import jax
import jax.numpy as jnp
from jax import lax

NO = 16
NV = 160


def draw_amplitudes(key, part):
    first_key = jax.random.fold_in(key, 11)
    initial = jax.random.normal(first_key, (NO, NO, NV, NV), jnp.float32)
    symmetric = (initial + initial.transpose(1, 0, 3, 2)) * 0.7071
    return jnp.clip(symmetric, -8.0, 8.0)


def shard_levels(key, dims, shards, least, high):
    loudness = 1.0
    for dim, blocks in shards:
        draws = jax.random.uniform(jax.random.fold_in(jax.random.fold_in(key, 6), dim), (blocks,), jnp.float32, least / len(shards), high / len(shards))
        loudness = loudness * jnp.repeat(jnp.exp(draws), dims[dim] // blocks).reshape((-1,) + (1,) * (len(dims) - 1 - dim))
    return loudness


def centred(stream_key, extent, scale, bound, pieces=(), dtype=jnp.bfloat16):
    gain = shard_levels(stream_key, extent, pieces, -0.22, 0.18) if pieces else 1.0
    array = jax.random.normal(stream_key, extent, jnp.float32) * scale * gain
    return jnp.minimum(jnp.maximum(array, -bound), bound).astype(dtype)


def setup_inputs(seed: int = 0) -> dict:
    keys = jax.random.split(jax.random.key(seed), 9)
    amplitudes = draw_amplitudes(jax.random.fold_in(keys[8], 71), 0)
    vvvv = centred(keys[1], (NV, NV, NV, NV), (NV * NV) ** -0.5, 0.0390625, ((0, 8), (2, 4)), jnp.float32)
    hole_ints = centred(keys[2], (NO, NO, NO, NO), (NO * NO) ** -0.5, 0.375, (), jnp.float32)
    exchange_ints = centred(keys[3], (NO, NO, NV, NV), (NO * NO * NV * NV) ** -0.5, 0.0024414062, ((0, 8), (2, 4)), jnp.float32)
    fock_occ = centred(keys[4], (NO, NO), NO ** -0.5, 1.5, (), jnp.float32)
    fock_vir = centred(keys[5], (NV, NV), NV ** -0.5, 0.5, (), jnp.float32)
    eps_occ = jnp.clip(jax.random.uniform(keys[6], (NO,), jnp.float32, -2.0, -0.5), -2.0, -0.5)
    eps_vir = jnp.clip(jax.random.uniform(keys[7], (NV,), jnp.float32, 0.3, 3.0), 0.3, 3.0)
    return {"amplitudes": amplitudes, "vvvv": vvvv, "hole_ints": hole_ints, "exchange_ints": exchange_ints, "fock_occ": fock_occ, "fock_vir": fock_vir, "eps_occ": eps_occ, "eps_vir": eps_vir}


def reference(amplitudes, vvvv, hole_ints, exchange_ints, fock_occ, fock_vir, eps_occ, eps_vir):
    highest = lax.Precision.HIGHEST
    matrix = amplitudes.reshape(NO * NO, NV * NV)
    ladder = lax.dot_general(matrix, vvvv.reshape(NV * NV, NV * NV), (((1,), (1,)), ((), ())), precision=highest)
    quadratic = lax.dot_general(matrix, exchange_ints.reshape(NO * NO, NV * NV), (((1,), (1,)), ((), ())), precision=highest)
    chi = hole_ints.reshape(NO * NO, NO * NO).T + quadratic
    hole = jnp.dot(chi, matrix, precision=highest)
    occupied_term = jnp.einsum("ikx,kj->ijx", amplitudes.reshape(NO, NO, NV * NV), fock_occ, precision=highest).reshape(NO * NO, NV * NV)
    raw = (ladder + hole - occupied_term).reshape(NO, NO, NV, NV)
    total = raw + raw.transpose(1, 0, 3, 2)
    total = total + jnp.einsum("ijac,cb->ijab", amplitudes, fock_vir, precision=highest)
    total = total + jnp.einsum("ac,ijcb->ijab", fock_vir, amplitudes, precision=highest)
    denominator = eps_occ[:, None, None, None] + eps_occ[None, :, None, None] - eps_vir[None, None, :, None] - eps_vir[None, None, None, :]
    return total / denominator
```

```python
import jax
import jax.numpy as jnp
from jax import lax
from jax.sharding import PartitionSpec as P

def on_device(amplitudes, vvvv, hole_ints, exchange_ints, fock_occ, fock_vir, eps_occ, eps_vir):
    high = lax.Precision.HIGH
    rows_n = lax.axis_size("row")
    cols_n = lax.axis_size("col")
    row = lax.axis_index("row")
    col = lax.axis_index("col")
    first_count, second_count, virtual = amplitudes.shape[:3]
    occupied = fock_occ.shape[0]
    pairs_n = occupied * occupied
    a_count = vvvv.shape[0]
    c_count = vvvv.shape[2]
    k_count = exchange_ints.shape[0]

    split = lax.all_to_all(amplitudes, "col", split_axis=2, concat_axis=1, tiled=True)
    split = split.reshape(first_count * occupied, c_count * virtual)
    gathered = lax.all_gather(split, "row", axis=0, tiled=True)
    gathered = gathered.reshape(occupied, occupied, c_count, virtual)

    chi_part = lax.dot_general(
        gathered, exchange_ints, (((2, 3), (2, 3)), ((), ())), precision=high
    )
    chi_part = chi_part.reshape(pairs_n, k_count * occupied).T
    chi_all = lax.all_gather(chi_part, ("row", "col"), axis=0)
    chi = chi_all.reshape(rows_n, cols_n, k_count * occupied, pairs_n).sum(axis=1)
    delta = jnp.eye(occupied, dtype=fock_occ.dtype)
    known = hole_ints - delta[:, None, :, None] * fock_occ[None, :, None, :]
    mixing = chi.reshape(pairs_n, pairs_n) + known.reshape(pairs_n, pairs_n)

    mine = lax.dynamic_slice_in_dim(gathered, row * a_count, a_count, axis=3)
    mine = mine.transpose(1, 0, 3, 2).reshape(pairs_n, a_count, c_count)
    placed = lax.dynamic_update_slice_in_dim(
        jnp.zeros((pairs_n, a_count, virtual), mine.dtype), mine, col * c_count, axis=2
    )

    part = lax.dot_general(gathered, vvvv, (((2, 3), (2, 3)), ((), ())), precision=high)
    hole = lax.dot_general(mixing, placed, (((0,), (0,)), ((), ())), precision=high)
    part = part + hole.reshape(part.shape)
    part = part.transpose(1, 0, 2, 3).reshape(occupied, occupied, a_count * virtual)
    raw = lax.psum_scatter(part, "col", scatter_dimension=0, tiled=True)
    raw = raw.reshape(second_count, rows_n, first_count, a_count * virtual)
    raw = raw.transpose(1, 2, 0, 3)
    raw = lax.all_to_all(raw, "row", split_axis=0, concat_axis=0, tiled=True)
    raw = raw.transpose(1, 2, 0, 3).reshape(first_count, second_count, virtual * virtual)

    ratio = second_count // first_count
    others = []
    for turn in range(ratio):
        route = []
        for r in range(rows_n):
            for q in range(cols_n):
                m = (r + turn) % ratio
                route.append((r * cols_n + q, (q * ratio + m) * cols_n + r // ratio))
        m = lax.rem(row + turn, ratio)
        block = lax.dynamic_slice_in_dim(raw, m * first_count, first_count, axis=1)
        others.append(lax.ppermute(block, ("row", "col"), route))
    stacked = jnp.stack(others)
    order = jnp.stack([lax.rem(row - m + ratio, ratio) for m in range(ratio)])
    other = stacked[order].reshape(ratio, first_count, first_count, virtual, virtual)
    other = other.transpose(2, 0, 1, 4, 3)
    other = other.reshape(first_count, second_count, virtual, virtual)
    total = raw.reshape(first_count, second_count, virtual, virtual) + other
    total = total + jnp.einsum("ijac,cb->ijab", amplitudes, fock_vir, precision=high)
    total = total + jnp.einsum("ac,ijcb->ijab", fock_vir, amplitudes, precision=high)
    energy_rows = lax.dynamic_slice_in_dim(eps_occ, row * first_count, first_count)
    energy_cols = lax.dynamic_slice_in_dim(eps_occ, col * second_count, second_count)
    denominator = (
        energy_rows[:, None, None, None]
        + energy_cols[None, :, None, None]
        - eps_vir[None, None, :, None]
        - eps_vir[None, None, None, :]
    )
    return total / denominator


def solution(mesh):
    in_specs = (
        P("row", "col", None, None),
        P("row", None, "col", None),
        P(),
        P("row", None, "col", None),
        P(),
        P(),
        P(),
        P(),
    )
    out_specs = P("row", "col", None, None)
    return jax.shard_map(
        on_device, mesh=mesh, in_specs=in_specs, out_specs=out_specs, check_vma=False
    )
```

```python
import jax
import jax.numpy as jnp
from jax import lax
from jax.sharding import PartitionSpec as P

def on_device(amplitudes, vvvv, hole_ints, exchange_ints, fock_occ, fock_vir, eps_occ, eps_vir):
    high = lax.Precision.HIGH
    rows_n = lax.axis_size("row")
    cols_n = lax.axis_size("col")
    row = lax.axis_index("row")
    col = lax.axis_index("col")
    first_count, second_count, virtual = amplitudes.shape[:3]
    occupied = fock_occ.shape[0]
    pairs_n = occupied * occupied
    a_count = vvvv.shape[0]
    c_count = vvvv.shape[2]
    k_count = exchange_ints.shape[0]

    split = lax.all_to_all(amplitudes, "col", split_axis=2, concat_axis=1, tiled=True)
    split = split.reshape(first_count * occupied, c_count * virtual)
    gathered = lax.all_gather(split, "row", axis=0, tiled=True)
    gathered = gathered.reshape(occupied, occupied, c_count, virtual)

    chi_part = lax.dot_general(
        gathered, exchange_ints, (((2, 3), (2, 3)), ((), ())), precision=high
    )
    chi_part = chi_part.reshape(pairs_n, k_count * occupied).T
    chi_all = lax.all_gather(chi_part, ("row", "col"), axis=0)
    chi = chi_all.reshape(rows_n, cols_n, k_count * occupied, pairs_n).sum(axis=1)
    delta = jnp.eye(occupied, dtype=fock_occ.dtype)
    known = hole_ints - delta[:, None, :, None] * fock_occ[None, :, None, :]
    mixing = chi.reshape(pairs_n, pairs_n) + known.reshape(pairs_n, pairs_n)

    mine = lax.dynamic_slice_in_dim(gathered, row * a_count, a_count, axis=3)
    mine = mine.transpose(1, 0, 3, 2).reshape(pairs_n, a_count * c_count)
    placed = lax.all_gather(mine, "col", axis=0)
    placed = placed.reshape(cols_n, pairs_n, a_count, c_count).transpose(1, 2, 0, 3)
    placed = placed.reshape(pairs_n, a_count * virtual)

    part = lax.dot_general(gathered, vvvv, (((2, 3), (2, 3)), ((), ())), precision=high)
    part = part.transpose(1, 0, 2, 3).reshape(occupied, occupied, a_count * virtual)
    raw = lax.psum_scatter(part, "col", scatter_dimension=0, tiled=True)
    chosen = lax.dynamic_slice_in_dim(
        mixing.reshape(pairs_n, occupied, occupied), col * second_count, second_count, axis=2
    )
    chosen = chosen.transpose(0, 2, 1).reshape(pairs_n, second_count * occupied)
    hole = lax.dot_general(chosen, placed, (((0,), (0,)), ((), ())), precision=high)
    raw = raw + hole.reshape(raw.shape)
    raw = raw.reshape(second_count, rows_n, first_count, a_count * virtual)
    raw = raw.transpose(1, 2, 0, 3)
    raw = lax.all_to_all(raw, "row", split_axis=0, concat_axis=0, tiled=True)
    raw = raw.transpose(1, 2, 0, 3).reshape(first_count, second_count, virtual * virtual)

    ratio = second_count // first_count
    others = []
    for turn in range(ratio):
        route = []
        for r in range(rows_n):
            for q in range(cols_n):
                m = (r + turn) % ratio
                route.append((r * cols_n + q, (q * ratio + m) * cols_n + r // ratio))
        m = lax.rem(row + turn, ratio)
        block = lax.dynamic_slice_in_dim(raw, m * first_count, first_count, axis=1)
        others.append(lax.ppermute(block, ("row", "col"), route))
    stacked = jnp.stack(others)
    order = jnp.stack([lax.rem(row - m + ratio, ratio) for m in range(ratio)])
    other = stacked[order].reshape(ratio, first_count, first_count, virtual, virtual)
    other = other.transpose(2, 0, 1, 4, 3)
    other = other.reshape(first_count, second_count, virtual, virtual)
    total = raw.reshape(first_count, second_count, virtual, virtual) + other
    total = total + jnp.einsum("ijac,cb->ijab", amplitudes, fock_vir, precision=high)
    total = total + jnp.einsum("ac,ijcb->ijab", fock_vir, amplitudes, precision=high)
    energy_rows = lax.dynamic_slice_in_dim(eps_occ, row * first_count, first_count)
    energy_cols = lax.dynamic_slice_in_dim(eps_occ, col * second_count, second_count)
    denominator = (
        energy_rows[:, None, None, None]
        + energy_cols[None, :, None, None]
        - eps_vir[None, None, :, None]
        - eps_vir[None, None, None, :]
    )
    return total / denominator


def solution(mesh):
    in_specs = (
        P("row", "col", None, None),
        P("row", None, "col", None),
        P(),
        P("row", None, "col", None),
        P(),
        P(),
        P(),
        P(),
    )
    out_specs = P("row", "col", None, None)
    return jax.shard_map(
        on_device, mesh=mesh, in_specs=in_specs, out_specs=out_specs, check_vma=False
    )
```
